128 devices in a mesh: blk: 32 (over x, y, z_hi), walk: 4 (over z_lo, core).
Axes of the slice: x: 4, y: 4, z: 4 (z_hi: 2, z_lo: 2; z = z_hi * 2 + z_lo), core: 2. Of those that a mesh axis runs over, the one named last changes fastest.
Arguments:
- walker_m: bfloat16 [4, 32, 128, 128], P('walk', 'blk'), may hold values from -6 to 6
- vertex_times: int32 [4, 32, 128], P('walk', 'blk'), may hold values from 0 to 1023
- vertex_labels: int32 [4, 32, 128], P('walk', 'blk'), may hold values from 0 to 35
- freq_index: int32 [24], replicated, may hold values from -64 to 63
- q_index: int32 [32], P('blk'), may hold values from 0 to 35
Outputs:
- g4: float32 [32, 2, 864, 864], P('blk', None, 'walk')
The draws below stay inside these ranges and needn't reach their ends.
Inputs may be any that keep to these rules, and one draw needn't show every extreme that they name: `q_index`: entry b is 6 qx + qy for the transfer momentum (qx, qy). `freq_index`: frequency f is pi (2 n + 1) / beta with n its entry. `vertex_times`: the time is entry * beta / 1024. `vertex_labels`: site s lies at row s // 6 and column s mod 6 of the 6×6 cluster.
All inputs are finite; a program needn't handle non-finite values.
Results may differ from the reference program's by a relative error of at most 0.0061.
Values may be sent and summed in bfloat16 or wider, within the bound.
No kernel may reach another device: no remote copies, remote signals or barrier semaphores. Data moves between devices by JAX's collectives and lax.ppermute only.
A program may use at most 128 MiB of HBM per device.

```python
import math
import jax
import jax.numpy as jnp
from jax import lax

SIDE = 6
NK = 36
NF = 24
K = 864
V = 128
STEPS = 4
TGRID = 1024
OWNERS = 32
GROUPS = 4
N_BLK = 32
N_WALK = 4


def touch_ends(drawn, key, low, high):
    dims = drawn.shape
    place = [jax.random.randint(jax.random.fold_in(key, axis), (), 0, dims[axis]) for axis in range(len(dims))]
    drawn = drawn.at[tuple(place)].set(low)
    longest = dims.index(max(dims))
    place[longest] = (place[longest] + 1) % dims[longest]
    return drawn.at[tuple(place)].set(high)


def block_levels(stream_key, dims, cuts, least, top_value):
    def one(dim, blocks):
        draws = jax.random.uniform(jax.random.fold_in(jax.random.fold_in(stream_key, 6), dim), (blocks,), jnp.float32, least / len(cuts), top_value / len(cuts))
        return jnp.repeat(jnp.exp(draws), dims[dim] // blocks).reshape((-1,) + (1,) * (len(dims) - dim - 1))

    factor_of = one(*cuts[0])
    for cut in cuts[1:]:
        factor_of = factor_of * one(*cut)
    return factor_of


def gaussian(stream_key, dims, width, reach, cuts=(), kind=jnp.bfloat16):
    loudness = block_levels(stream_key, dims, cuts, -0.22, 0.18) if cuts else 1.0
    values = jax.random.normal(stream_key, dims, jnp.float32) * width * loudness
    return jnp.minimum(jnp.maximum(values, -reach), reach).astype(kind)


def setup_inputs(seed: int = 0) -> dict:
    streams_of = jax.random.split(jax.random.key(seed), 6)
    return {
        "walker_m": gaussian(streams_of[0], (GROUPS, OWNERS, V, V), 1.0, 6.0, ((0, 4), (1, 32))),
        "vertex_times": touch_ends(jax.random.randint(streams_of[1], (GROUPS, OWNERS, V), 0, TGRID), jax.random.fold_in(streams_of[1], 1), 0, TGRID - 1).astype(jnp.int32),
        "vertex_labels": touch_ends(jax.random.randint(streams_of[2], (GROUPS, OWNERS, V), 0, NK), jax.random.fold_in(streams_of[2], 1), 0, NK - 1).astype(jnp.int32),
        "freq_index": touch_ends(jax.random.randint(streams_of[3], (NF,), -64, 64), jax.random.fold_in(streams_of[3], 1), -64, 63).astype(jnp.int32),
        "q_index": touch_ends(jax.random.randint(streams_of[4], (OWNERS,), 0, NK), jax.random.fold_in(streams_of[4], 1), 0, NK - 1).astype(jnp.int32),
    }


TWO_PI = 2.0 * math.pi


def phase_tables(time_points, labels, frequencies):
    modulus = 12 * TGRID
    momenta = jnp.arange(NK, dtype=jnp.int32)
    momentum_across = momenta // SIDE
    momentum_down = momenta % SIDE
    site_across = labels // SIDE
    site_down = labels % SIDE
    freq_part = jnp.mod((2 * frequencies[:, None] + 1) * time_points[None, :] * 6, modulus)
    momentum_part = jnp.mod(2 * TGRID * (momentum_across[:, None] * site_across[None, :] + momentum_down[:, None] * site_down[None, :]), modulus)
    phase = jnp.mod(freq_part[None, :, :] - momentum_part[:, None, :], modulus).reshape(NK * NF, -1)
    angles = phase.astype(jnp.float32) * (TWO_PI / modulus)
    return jnp.cos(angles).astype(jnp.bfloat16), jnp.sin(angles).astype(jnp.bfloat16)


def build_green(matrix, time_points, labels, frequencies):
    cos_table, sin_table = phase_tables(time_points, labels, frequencies)
    stacked = jnp.concatenate([cos_table, sin_table], axis=0)
    amplitude = jnp.dot(stacked, matrix, preferred_element_type=jnp.float32).astype(jnp.bfloat16)
    real_part = amplitude[:K]
    imag_part = amplitude[K:]
    left_side = jnp.concatenate([jnp.concatenate([real_part, imag_part], axis=1), jnp.concatenate([imag_part, -real_part], axis=1)], axis=0)
    right_side = jnp.concatenate([cos_table, sin_table], axis=1)
    green_table = lax.dot_general(left_side, right_side, (((1,), (1,)), ((), ())), preferred_element_type=jnp.float32)
    return (green_table * (1.0 / V)).reshape(2, K, K)


def shifted_rows(transfer):
    transfer = transfer.astype(jnp.int32)
    row_index = jnp.arange(K, dtype=jnp.int32)
    momentum = row_index // NF
    offset = row_index % NF
    shift_across = (momentum // SIDE + transfer // SIDE) % SIDE
    shift_down = (momentum % SIDE + transfer % SIDE) % SIDE
    return ((shift_across * SIDE + shift_down) * NF + offset).astype(jnp.int32)


def contribution(green_table, shifted):
    shifted_green = jnp.take(jnp.take(green_table, shifted, axis=1), shifted, axis=2)
    flipped = jnp.swapaxes(green_table, 1, 2)
    real_term = shifted_green[0] * flipped[0] - shifted_green[1] * flipped[1]
    imag_term = shifted_green[0] * flipped[1] + shifted_green[1] * flipped[0]
    return jnp.stack([real_term, imag_term])


def reference(walker_m, vertex_times, vertex_labels, freq_index, q_index):
    walker_count = N_WALK * N_BLK
    matrices = walker_m.reshape(walker_count, V, V)
    time_rows = vertex_times.reshape(walker_count, V)
    label_rows = vertex_labels.reshape(walker_count, V)
    sources = jnp.arange(walker_count, dtype=jnp.int32) % N_BLK

    def visit_walker(running, walker_item):
        matrix, time_points, labels, source = walker_item
        green_table = build_green(matrix, time_points, labels, freq_index)
        for number in range(STEPS):
            offset = number - (STEPS // 2 - 1)
            owner_index = jnp.mod(source - offset, N_BLK).astype(jnp.int32)
            addition = contribution(green_table, shifted_rows(q_index[owner_index]))
            running = running.at[owner_index].add(addition)
        return running, None

    start = jnp.zeros((N_BLK, 2, K, K), jnp.float32)
    running, unused = lax.scan(visit_walker, start, (matrices, time_rows, label_rows, sources))
    return running * (1.0 / (STEPS * N_WALK))
```

```python
import jax
import jax.numpy as jnp
from jax import lax
from jax.experimental import pallas as pl
from jax.experimental.pallas import tpu as pltpu
from jax.sharding import PartitionSpec as P

SIDE = 6
NF = 24
K = 864
V = 128
STEPS = 4
ROWS = 216
PACK = 144
BLOCKS = 9
COL_TILES = ((0, 256), (256, 256), (512, 256), (768, 96))


def quarter_cos_sin(turns):
    near = jnp.floor(turns + 0.5)
    x = turns - near
    x2 = x * x
    s = x * (1.5707963267948966 + x2 * (-0.6459640975062462 + x2 * (0.07969262624616704 + x2 * (-0.004681754135318688 + x2 * 0.00016044118478735982))))
    c = 1.0 + x2 * (-1.2337005501361697 + x2 * (0.253669507901048 + x2 * (-0.02086348076335296 + x2 * (0.0009192602748394266 + x2 * -2.520204237306061e-05))))
    quad = near - 4.0 * jnp.floor(near * 0.25)
    odd = (quad == 1.0) | (quad == 3.0)
    cc = jnp.where(odd, s, c)
    ss = jnp.where(odd, c, s)
    cc = jnp.where((quad == 1.0) | (quad == 2.0), -cc, cc)
    ss = jnp.where(quad >= 2.0, -ss, ss)
    return cc, ss


def sixth_cos_sin(m):
    y = m - 6.0 * jnp.floor((m + 0.5) * (1.0 / 6.0))
    z = jnp.abs(y - 3.0)
    half = 0.8660254037844386
    c = jnp.where(z == 3.0, 1.0, jnp.where(z == 2.0, 0.5, jnp.where(z == 1.0, -0.5, -1.0)))
    s = jnp.where((z == 3.0) | (z == 0.0), 0.0, jnp.where(y < 3.0, half, -half))
    return c, s


def walker_kernel(place_ref, odd_freq_ref, walkers_ref, out_ref, table_ref, left_ref):
    step = pl.program_id(0)
    share, transfer = place_ref[0], place_ref[1]
    packed = walkers_ref[0]
    meta = packed[V:, :].astype(jnp.float32)
    times = meta[0:1] * 32.0 + meta[1:2]
    sites = meta[2:3]
    site_x = jnp.floor((sites + 0.5) * (1.0 / SIDE))
    site_y = sites - SIDE * site_x
    product = odd_freq_ref[...] * times
    freq_c, freq_s = quarter_cos_sin((product - 2048.0 * jnp.floor(product * (1.0 / 2048.0))) * (1.0 / 512.0))

    def rows_of(kx, ky):
        return sixth_cos_sin(kx * site_x + ky * site_y)

    index = lax.broadcasted_iota(jnp.int32, (16, V), 0)
    base_c, base_s = rows_of((index // 3).astype(jnp.float32), (index % 3).astype(jnp.float32))
    mine = index + BLOCKS * share
    mine_x = (mine // SIDE).astype(jnp.float32)
    mine_y = (mine % SIDE).astype(jnp.float32)
    q_x = (transfer // SIDE).astype(jnp.float32)
    q_y = (transfer % SIDE).astype(jnp.float32)
    mine_c, mine_s = rows_of(mine_x, mine_y)
    moved_c, moved_s = rows_of(mine_x + q_x, mine_y + q_y)
    turn_c, turn_s = rows_of(q_x, q_y)
    flip_x = 1.0 - 2.0 * (site_x - 2.0 * jnp.floor(site_x * 0.5))
    flip_y = 1.0 - 2.0 * (site_y - 2.0 * jnp.floor(site_y * 0.5))

    def rotated(c, s, row):
        c, s = c[row : row + 1], s[row : row + 1]
        return freq_c * c + freq_s * s, freq_s * c - freq_c * s

    for kx in range(3):
        blocks = [rotated(base_c, base_s, 3 * kx + ky) for ky in range(3)]
        blocks = blocks + [(c * flip_y, s * flip_y) for c, s in blocks]
        cos_part = jnp.concatenate([b[0] for b in blocks], axis=0).astype(jnp.bfloat16)
        sin_part = jnp.concatenate([b[1] for b in blocks], axis=0).astype(jnp.bfloat16)
        flip = flip_x.astype(jnp.bfloat16)
        table_ref[pl.ds(144 * kx, 144), 0:V] = cos_part
        table_ref[pl.ds(144 * kx, 144), V:] = sin_part
        table_ref[pl.ds(144 * (kx + 3), 144), 0:V] = cos_part * flip
        table_ref[pl.ds(144 * (kx + 3), 144), V:] = sin_part * flip

    def stacked(c, s):
        blocks = [rotated(c, s, j) for j in range(BLOCKS)]
        return jnp.concatenate([b[0] for b in blocks] + [b[1] for b in blocks], axis=0).astype(jnp.bfloat16)

    matrix = packed[:V, :]
    first = jnp.dot(stacked(moved_c, moved_s), matrix, preferred_element_type=jnp.float32)
    second = lax.dot_general(stacked(mine_c, mine_s), matrix, (((1,), (1,)), ((), ())), preferred_element_type=jnp.float32)
    a_re, a_im = first[:ROWS], first[ROWS:]
    turn_c, turn_s = turn_c[0:1], turn_s[0:1]
    a_re, a_im = a_re * turn_c - a_im * turn_s, a_re * turn_s + a_im * turn_c
    b_re, b_im = second[:ROWS], second[ROWS:]

    def interleave(parts):
        return jnp.stack([p.reshape(27, 8, V) for p in parts], axis=1).reshape(K, V).astype(jnp.bfloat16)

    left_ref[:, 0:V] = interleave([a_re, a_im, b_re, -b_im])
    left_ref[:, V:] = interleave([a_im, -a_re, b_im, b_re])

    @pl.when(step == 0)
    def _():
        out_ref[...] = jnp.zeros_like(out_ref)

    for start, size in COL_TILES:
        product = lax.dot_general(left_ref[...], table_ref[pl.ds(start, size), :], (((1,), (1,)), ((), ())), preferred_element_type=jnp.float32)
        product = product.reshape(27, 4, 8, size)
        m_re, m_im, n_re, n_im = (product[:, i] for i in range(4))
        out_ref[0, :, pl.ds(start, size)] += (m_re * n_re - m_im * n_im).reshape(ROWS, size)
        out_ref[1, :, pl.ds(start, size)] += (m_re * n_im + m_im * n_re).reshape(ROWS, size)

    @pl.when(step == pl.num_programs(0) - 1)
    def _():
        out_ref[...] = out_ref[...] * (2.0 ** -18)


def accumulate(place, odd_freq, walkers):
    return pl.pallas_call(
        walker_kernel,
        out_shape=jax.ShapeDtypeStruct((2, ROWS, K), jnp.float32),
        grid_spec=pltpu.PrefetchScalarGridSpec(
            num_scalar_prefetch=1,
            grid=(walkers.shape[0],),
            in_specs=[
                pl.BlockSpec((NF, V), lambda i, p: (0, 0)),
                pl.BlockSpec((1, PACK, V), lambda i, p: (i, 0, 0)),
            ],
            out_specs=pl.BlockSpec((2, ROWS, K), lambda i, p: (0, 0, 0)),
            scratch_shapes=[pltpu.VMEM((K, 256), jnp.bfloat16), pltpu.VMEM((K, 256), jnp.bfloat16)],
        ),
        compiler_params=pltpu.CompilerParams(vmem_limit_bytes=48 << 20),
    )(place, odd_freq, walkers)


def shifted_owner(value, steps):
    count = lax.axis_size("blk")
    return lax.ppermute(value, "blk", [((i + steps) % count, i) for i in range(count)])


def local(walker_m, vertex_times, vertex_labels, freq_index, q_index):
    times, labels = vertex_times[0], vertex_labels[0]
    meta = jnp.concatenate([times // 32, times % 32, labels], axis=0).astype(jnp.bfloat16)
    packed = jnp.concatenate([walker_m[0, 0], meta, jnp.zeros((PACK - V - 3, V), jnp.bfloat16)], axis=0)
    groups = lax.all_gather(packed, "walk", axis=0)
    walkers = jnp.concatenate([groups] + [shifted_owner(groups, d) for d in (-1, 1, 2)], axis=0)
    place = jnp.stack([lax.axis_index("walk").astype(jnp.int32), q_index[0]])
    odd_freq = jnp.broadcast_to((2 * freq_index + 1).astype(jnp.float32)[:, None], (NF, V))
    return accumulate(place, odd_freq, walkers)[None]


def solution(mesh):
    return jax.shard_map(
        local,
        mesh=mesh,
        in_specs=(
            P("walk", "blk", None, None),
            P("walk", "blk", None),
            P("walk", "blk", None),
            P(),
            P("blk"),
        ),
        out_specs=P("blk", None, "walk", None),
        check_vma=False,
    )
```

```python
import jax
import jax.numpy as jnp
from jax import lax
from jax.experimental import pallas as pl
from jax.experimental.pallas import tpu as pltpu
from jax.sharding import Mesh
from jax.sharding import PartitionSpec as P

SIDE = 6
NF = 24
K = 864
V = 128
STEPS = 4
ROWS = 216
PACK = 136
BLOCKS = 9
COL_TILES = ((0, 256), (256, 256), (512, 256), (768, 96))


def quarter_cos_sin(turns):
    near = jnp.floor(turns + 0.5)
    x = turns - near
    x2 = x * x
    s = x * (1.5707963267948966 + x2 * (-0.6459640975062462 + x2 * (0.07969262624616704 + x2 * (-0.004681754135318688 + x2 * 0.00016044118478735982))))
    c = 1.0 + x2 * (-1.2337005501361697 + x2 * (0.253669507901048 + x2 * (-0.02086348076335296 + x2 * (0.0009192602748394266 + x2 * -2.520204237306061e-05))))
    quad = near - 4.0 * jnp.floor(near * 0.25)
    odd = (quad == 1.0) | (quad == 3.0)
    cc = jnp.where(odd, s, c)
    ss = jnp.where(odd, c, s)
    cc = jnp.where((quad == 1.0) | (quad == 2.0), -cc, cc)
    ss = jnp.where(quad >= 2.0, -ss, ss)
    return cc, ss


def sixth_cos_sin(m):
    y = m - 6.0 * jnp.floor((m + 0.5) * (1.0 / 6.0))
    z = jnp.abs(y - 3.0)
    half = 0.8660254037844386
    c = jnp.where(z == 3.0, 1.0, jnp.where(z == 2.0, 0.5, jnp.where(z == 1.0, -0.5, -1.0)))
    s = jnp.where((z == 3.0) | (z == 0.0), 0.0, jnp.where(y < 3.0, half, -half))
    return c, s


def pieces(share, transfer, odd_freq_ref, walkers_ref, w, table_ref, left_ref):
    st = {}

    def rotated(c, s, row):
        c, s = c[row : row + 1], s[row : row + 1]
        fc, fs = st["f"]
        return fc * c + fs * s, fs * c - fc * s

    def stacked(c, s):
        blocks = [rotated(c, s, j) for j in range(BLOCKS)]
        return jnp.concatenate([b[0] for b in blocks] + [b[1] for b in blocks], axis=0).astype(jnp.bfloat16)

    def interleave(parts):
        return jnp.stack([p.reshape(27, 8, V) for p in parts], axis=1).reshape(K, V).astype(jnp.bfloat16)

    def p0():
        meta = walkers_ref[w, V:, :].astype(jnp.float32)
        times = meta[0:1] * 32.0 + meta[1:2]
        sites = meta[2:3]
        site_x = jnp.floor((sites + 0.5) * (1.0 / SIDE))
        site_y = sites - SIDE * site_x
        product = odd_freq_ref[...] * times
        st["f"] = quarter_cos_sin((product - 2048.0 * jnp.floor(product * (1.0 / 2048.0))) * (1.0 / 512.0))

        def rows_of(kx, ky):
            return sixth_cos_sin(kx * site_x + ky * site_y)

        index = lax.broadcasted_iota(jnp.int32, (16, V), 0)
        st["base"] = rows_of((index // 3).astype(jnp.float32), (index % 3).astype(jnp.float32))
        mine = index + BLOCKS * share
        mine_x = (mine // SIDE).astype(jnp.float32)
        mine_y = (mine % SIDE).astype(jnp.float32)
        q_x = (transfer // SIDE).astype(jnp.float32)
        q_y = (transfer % SIDE).astype(jnp.float32)
        moved = rows_of(mine_x + q_x, mine_y + q_y)
        mine = rows_of(mine_x, mine_y)
        turn_c, turn_s = rows_of(q_x, q_y)
        st["turn"] = turn_c[0:1] * (2.0 ** -18), turn_s[0:1] * (2.0 ** -18)
        st["flip_x"] = 1.0 - 2.0 * (site_x - 2.0 * jnp.floor(site_x * 0.5))
        st["flip_y"] = 1.0 - 2.0 * (site_y - 2.0 * jnp.floor(site_y * 0.5))
        matrix = walkers_ref[w, :V, :]
        st["first"] = jnp.dot(stacked(*moved), matrix, preferred_element_type=jnp.float32)
        st["second"] = lax.dot_general(stacked(*mine), matrix, (((1,), (1,)), ((), ())), preferred_element_type=jnp.float32)

    def p1():
        base_c, base_s = st["base"]
        flip_x, flip_y = st["flip_x"], st["flip_y"]
        for kx in range(3):
            blocks = [rotated(base_c, base_s, 3 * kx + ky) for ky in range(3)]
            blocks = blocks + [(c * flip_y, s * flip_y) for c, s in blocks]
            cos_part = jnp.concatenate([b[0] for b in blocks], axis=0).astype(jnp.bfloat16)
            sin_part = jnp.concatenate([b[1] for b in blocks], axis=0).astype(jnp.bfloat16)
            flip = flip_x.astype(jnp.bfloat16)
            table_ref[pl.ds(144 * kx, 144), 0:V] = cos_part
            table_ref[pl.ds(144 * kx, 144), V:] = sin_part
            table_ref[pl.ds(144 * (kx + 3), 144), 0:V] = cos_part * flip
            table_ref[pl.ds(144 * (kx + 3), 144), V:] = sin_part * flip

    def p2():
        first = st["first"]
        a_re, a_im = first[:ROWS], first[ROWS:]
        turn_c, turn_s = st["turn"]
        st["a"] = a_re * turn_c - a_im * turn_s, a_re * turn_s + a_im * turn_c
        second = st["second"]
        a_re, a_im = st["a"]
        b_re, b_im = second[:ROWS], second[ROWS:]
        left_ref[:, 0:V] = interleave([a_re, a_im, b_re, -b_im])
        left_ref[:, V:] = interleave([a_im, -a_re, b_im, b_re])

    return [p0, p1, p2]


def tile_main(t, table_ref, left_ref, acc_ref):
    start, size = COL_TILES[t]
    product = lax.dot_general(left_ref[...], table_ref[pl.ds(start, size), :], (((1,), (1,)), ((), ())), preferred_element_type=jnp.float32)
    product = product.reshape(27, 4, 8, size)
    m_re, m_im, n_re, n_im = (product[:, i] for i in range(4))
    acc_ref[0, :, pl.ds(start, size)] += (m_re * n_re - m_im * n_im).reshape(ROWS, size)
    acc_ref[1, :, pl.ds(start, size)] += (m_re * n_im + m_im * n_re).reshape(ROWS, size)


def pack_kernel(freq_hbm, matrix_hbm, times_hbm, labels_hbm, packed_ref, odd_freq_ref, freq_ref, times_ref, labels_ref, sem):
    copies = (
        pltpu.make_async_copy(matrix_hbm.at[0], packed_ref.at[:, pl.ds(0, V), :], sem.at[0]),
        pltpu.make_async_copy(times_hbm, times_ref, sem.at[1]),
        pltpu.make_async_copy(labels_hbm, labels_ref, sem.at[2]),
        pltpu.make_async_copy(freq_hbm, freq_ref, sem.at[3]),
    )
    for copy in copies:
        copy.start()
    for copy in copies[1:]:
        copy.wait()
    row = lax.broadcasted_iota(jnp.int32, (PACK - V, V), 0)
    times = jnp.broadcast_to(times_ref[0], (PACK - V, V))
    labels = jnp.broadcast_to(labels_ref[0], (PACK - V, V))
    meta = jnp.where(row == 0, times // 32, jnp.where(row == 1, times % 32, jnp.where(row == 2, labels, 0)))
    packed_ref[0, V:, :] = meta.astype(jnp.float32).astype(jnp.bfloat16)
    row = lax.broadcasted_iota(jnp.int32, (NF, V), 0)
    odd = jnp.zeros((NF, V), jnp.int32)
    for f in range(NF):
        odd = jnp.where(row == f, 2 * freq_ref[f] + 1, odd)
    odd_freq_ref[...] = odd.astype(jnp.float32)
    copies[0].wait()


def pack(freq_index, matrix, times, labels):
    vmem = pl.BlockSpec(memory_space=pltpu.VMEM)
    return pl.pallas_call(
        pack_kernel,
        out_shape=(
            jax.ShapeDtypeStruct((1, PACK, V), jnp.bfloat16),
            jax.ShapeDtypeStruct((NF, V), jnp.float32),
        ),
        in_specs=[pl.BlockSpec(memory_space=pl.ANY)] * 4,
        out_specs=(vmem, vmem),
        scratch_shapes=[
            pltpu.SMEM((NF,), jnp.int32),
            pltpu.VMEM((1, 1, V), jnp.int32),
            pltpu.VMEM((1, 1, V), jnp.int32),
            pltpu.SemaphoreType.DMA((4,)),
        ],
        compiler_params=pltpu.CompilerParams(vmem_limit_bytes=4 << 20),
        name="pack",
    )(*(pltpu.with_memory_space_constraint(x, pltpu.HBM) for x in (freq_index, matrix, times, labels)))


def absorb_kernel(first, final, share_ref, transfer_ref, odd_freq_ref, walkers_ref, *refs):
    if first:
        acc_ref, *refs = refs
    else:
        old_ref, acc_ref, *refs = refs
    if final:
        out_ref, *refs = refs
    table_a, left_a, table_b, left_b, sem = refs
    n = walkers_ref.shape[0]
    place = share_ref[0], transfer_ref[0], odd_freq_ref, walkers_ref
    if first:
        acc_ref[...] = jnp.zeros_like(acc_ref)
    for piece in pieces(*place, 0, table_a, left_a):
        piece()

    def copy(tile):
        cols = pl.ds(*COL_TILES[tile])
        return pltpu.make_async_copy(acc_ref.at[:, :, cols], out_ref.at[:, :, cols], sem.at[tile])

    def half(current, following, following_walker, last=False):
        todo = [] if following is None else pieces(*place, following_walker, *following)
        for tile in range(4):
            tile_main(tile, *current, acc_ref)
            if last:
                copy(tile).start()
            if tile < len(todo):
                todo[tile]()

    slot_a, slot_b = (table_a, left_a), (table_b, left_b)

    def body(i, carry):
        half(slot_a, slot_b, 2 * i + 1)
        half(slot_b, slot_a, 2 * i + 2)
        return carry

    if n > 2:
        lax.fori_loop(0, n // 2 - 1, body, 0)
    half(slot_a, slot_b, n - 1)
    half(slot_b, None, None, last=final)
    if final:
        for tile in range(4):
            copy(tile).wait()


def absorb(share, transfer, odd_freq, walkers, acc=None, final=False):
    n = walkers.shape[0]
    vmem = pl.BlockSpec(memory_space=pltpu.VMEM)
    smem = pl.BlockSpec(memory_space=pltpu.SMEM)
    total = jax.ShapeDtypeStruct((2, ROWS, K), jnp.float32)
    args = [share, transfer, odd_freq, walkers] + ([] if acc is None else [acc])
    result = pl.pallas_call(
        lambda *refs: absorb_kernel(acc is None, final, *refs),
        out_shape=(total, total) if final else (total,),
        in_specs=[smem, smem] + [vmem] * (len(args) - 2),
        out_specs=(vmem, pl.BlockSpec(memory_space=pl.ANY)) if final else (vmem,),
        scratch_shapes=[pltpu.VMEM((K, 256), jnp.bfloat16)] * 4 + [pltpu.SemaphoreType.DMA((4,))],
        input_output_aliases={} if acc is None else {4: 0},
        cost_estimate=pl.CostEstimate(flops=n * 450_000_000, bytes_accessed=n * 40_000, transcendentals=0),
        compiler_params=pltpu.CompilerParams(vmem_limit_bytes=16 << 20),
        name="absorb",
    )(*args)
    return result[-1]


COORDS = ("x", "y", "zh", "zl", "core")


def permute(value, source):
    pairs = []
    for target in range(128):
        x, y, zh, zl, core = target // 32, target // 8 % 4, target // 4 % 2, target // 2 % 2, target % 2
        place = source(x, y, zh, zl, core)
        if place is not None:
            x, y, zh, zl, core = place
            pairs.append(((((x * 4 + y) * 2 + zh) * 2 + zl) * 2 + core, target))
    return lax.ppermute(value, COORDS, pairs)


def owner_at(steps):
    def source(x, y, zh, zl, core):
        owner = ((x * 4 + y) * 2 + zh + steps) % 32
        return owner // 8, owner // 2 % 4, owner % 2, zl, core

    return source


def local(walker_m, vertex_times, vertex_labels, freq_index, q_index):
    own, odd_freq = pack(freq_index, walker_m, vertex_times, vertex_labels)
    share = (2 * lax.axis_index("zl") + lax.axis_index("core")).astype(jnp.int32).reshape(1)
    ahead = permute(own, owner_at(2))
    behind = permute(own, lambda x, y, zh, zl, core: owner_at(-2)(x, y, zh, zl, core) if zh == 1 else None)
    odd_owner = lax.axis_index("zh") == 1
    send = jnp.concatenate([own, jnp.where(odd_owner, behind, ahead)], axis=0)
    other = permute(send, lambda x, y, zh, zl, core: (x, y, 1 - zh, zl, core))
    group = jnp.concatenate([own, ahead, other], axis=0)
    near = permute(group, lambda x, y, zh, zl, core: (x, y, zh, 1 - zl, core))
    acc = absorb(share, q_index, odd_freq, group)
    near, acc = lax.optimization_barrier((near, acc))
    far = permute(jnp.concatenate([group, near], axis=0), lambda x, y, zh, zl, core: (x, y, zh, zl, 1 - core))
    acc = absorb(share, q_index, odd_freq, near, acc)
    out = absorb(share, q_index, odd_freq, far, acc, final=True)
    return out[None]


def solution(mesh):
    fine = Mesh(mesh.devices.reshape(4, 4, 2, 2, 2), COORDS)
    walk, blk = ("zl", "core"), ("x", "y", "zh")
    return jax.shard_map(
        local,
        mesh=fine,
        in_specs=(P(walk, blk, None, None), P(walk, blk, None), P(walk, blk, None), P(), P(blk)),
        out_specs=P(blk, None, walk, None),
        check_vma=False,
    )
```

```python
import jax
import jax.numpy as jnp
from jax import lax
from jax.experimental import pallas as pl
from jax.experimental.pallas import tpu as pltpu
from jax.sharding import Mesh
from jax.sharding import PartitionSpec as P

SIDE = 6
NF = 24
K = 864
V = 128
STEPS = 4
ROWS = 216
PACK = 136
BLOCKS = 9
COL_TILES = ((0, 256), (256, 256), (512, 256), (768, 96))


def quarter_cos_sin(turns):
    near = jnp.floor(turns + 0.5)
    x = turns - near
    x2 = x * x
    s = x * (1.5707963267948966 + x2 * (-0.6459640975062462 + x2 * (0.07969262624616704 + x2 * (-0.004681754135318688 + x2 * 0.00016044118478735982))))
    c = 1.0 + x2 * (-1.2337005501361697 + x2 * (0.253669507901048 + x2 * (-0.02086348076335296 + x2 * (0.0009192602748394266 + x2 * -2.520204237306061e-05))))
    quad = near - 4.0 * jnp.floor(near * 0.25)
    odd = (quad == 1.0) | (quad == 3.0)
    cc = jnp.where(odd, s, c)
    ss = jnp.where(odd, c, s)
    cc = jnp.where((quad == 1.0) | (quad == 2.0), -cc, cc)
    ss = jnp.where(quad >= 2.0, -ss, ss)
    return cc, ss


def sixth_cos_sin(m):
    y = m - 6.0 * jnp.floor((m + 0.5) * (1.0 / 6.0))
    z = jnp.abs(y - 3.0)
    half = 0.8660254037844386
    c = jnp.where(z == 3.0, 1.0, jnp.where(z == 2.0, 0.5, jnp.where(z == 1.0, -0.5, -1.0)))
    s = jnp.where((z == 3.0) | (z == 0.0), 0.0, jnp.where(y < 3.0, half, -half))
    return c, s


def pieces(share, transfer, odd_freq_ref, walkers_ref, w, table_ref, left_ref):
    st = {}

    def rotated(c, s, row):
        c, s = c[row : row + 1], s[row : row + 1]
        fc, fs = st["f"]
        return fc * c + fs * s, fs * c - fc * s

    def stacked(c, s):
        blocks = [rotated(c, s, j) for j in range(BLOCKS)]
        return jnp.concatenate([b[0] for b in blocks] + [b[1] for b in blocks], axis=0).astype(jnp.bfloat16)

    def interleave(parts):
        return jnp.stack([p.reshape(27, 8, V) for p in parts], axis=1).reshape(K, V).astype(jnp.bfloat16)

    def p0():
        meta = walkers_ref[w, V:, :].astype(jnp.float32)
        times = meta[0:1] * 32.0 + meta[1:2]
        sites = meta[2:3]
        site_x = jnp.floor((sites + 0.5) * (1.0 / SIDE))
        site_y = sites - SIDE * site_x
        product = odd_freq_ref[...] * times
        st["f"] = quarter_cos_sin((product - 2048.0 * jnp.floor(product * (1.0 / 2048.0))) * (1.0 / 512.0))

        def rows_of(kx, ky):
            return sixth_cos_sin(kx * site_x + ky * site_y)

        index = lax.broadcasted_iota(jnp.int32, (16, V), 0)
        st["base"] = rows_of((index // 3).astype(jnp.float32), (index % 3).astype(jnp.float32))
        mine = index + BLOCKS * share
        mine_x = (mine // SIDE).astype(jnp.float32)
        mine_y = (mine % SIDE).astype(jnp.float32)
        q_x = (transfer // SIDE).astype(jnp.float32)
        q_y = (transfer % SIDE).astype(jnp.float32)
        moved = rows_of(mine_x + q_x, mine_y + q_y)
        mine = rows_of(mine_x, mine_y)
        turn_c, turn_s = rows_of(q_x, q_y)
        st["turn"] = turn_c[0:1] * (2.0 ** -18), turn_s[0:1] * (2.0 ** -18)
        st["flip_x"] = 1.0 - 2.0 * (site_x - 2.0 * jnp.floor(site_x * 0.5))
        st["flip_y"] = 1.0 - 2.0 * (site_y - 2.0 * jnp.floor(site_y * 0.5))
        matrix = walkers_ref[w, :V, :]
        st["first"] = jnp.dot(stacked(*moved), matrix, preferred_element_type=jnp.float32)
        st["second"] = lax.dot_general(stacked(*mine), matrix, (((1,), (1,)), ((), ())), preferred_element_type=jnp.float32)

    def p1():
        base_c, base_s = st["base"]
        flip_x, flip_y = st["flip_x"], st["flip_y"]
        for kx in range(3):
            blocks = [rotated(base_c, base_s, 3 * kx + ky) for ky in range(3)]
            blocks = blocks + [(c * flip_y, s * flip_y) for c, s in blocks]
            cos_part = jnp.concatenate([b[0] for b in blocks], axis=0).astype(jnp.bfloat16)
            sin_part = jnp.concatenate([b[1] for b in blocks], axis=0).astype(jnp.bfloat16)
            flip = flip_x.astype(jnp.bfloat16)
            table_ref[pl.ds(144 * kx, 144), 0:V] = cos_part
            table_ref[pl.ds(144 * kx, 144), V:] = sin_part
            table_ref[pl.ds(144 * (kx + 3), 144), 0:V] = cos_part * flip
            table_ref[pl.ds(144 * (kx + 3), 144), V:] = sin_part * flip

    def p2():
        first = st["first"]
        a_re, a_im = first[:ROWS], first[ROWS:]
        turn_c, turn_s = st["turn"]
        st["a"] = a_re * turn_c - a_im * turn_s, a_re * turn_s + a_im * turn_c
        second = st["second"]
        a_re, a_im = st["a"]
        b_re, b_im = second[:ROWS], second[ROWS:]
        left_ref[:, 0:V] = interleave([a_re, a_im, b_re, -b_im])
        left_ref[:, V:] = interleave([a_im, -a_re, b_im, b_re])

    return [p0, p1, p2]


def tile_main(t, table_ref, left_ref, acc_ref):
    start, size = COL_TILES[t]
    product = lax.dot_general(left_ref[...], table_ref[pl.ds(start, size), :], (((1,), (1,)), ((), ())), preferred_element_type=jnp.float32)
    product = product.reshape(27, 4, 8, size)
    m_re, m_im, n_re, n_im = (product[:, i] for i in range(4))
    acc_ref[0, :, pl.ds(start, size)] += (m_re * n_re - m_im * n_im).reshape(ROWS, size)
    acc_ref[1, :, pl.ds(start, size)] += (m_re * n_im + m_im * n_re).reshape(ROWS, size)


def pack_kernel(freq_hbm, matrix_hbm, times_hbm, labels_hbm, packed_ref, odd_freq_ref, freq_ref, times_ref, labels_ref, sem):
    copies = (
        pltpu.make_async_copy(matrix_hbm.at[0], packed_ref.at[:, pl.ds(0, V), :], sem.at[0]),
        pltpu.make_async_copy(times_hbm, times_ref, sem.at[1]),
        pltpu.make_async_copy(labels_hbm, labels_ref, sem.at[2]),
        pltpu.make_async_copy(freq_hbm, freq_ref, sem.at[3]),
    )
    for copy in copies:
        copy.start()
    for copy in copies[1:]:
        copy.wait()
    row = lax.broadcasted_iota(jnp.int32, (PACK - V, V), 0)
    times = jnp.broadcast_to(times_ref[0], (PACK - V, V))
    labels = jnp.broadcast_to(labels_ref[0], (PACK - V, V))
    meta = jnp.where(row == 0, times // 32, jnp.where(row == 1, times % 32, jnp.where(row == 2, labels, 0)))
    packed_ref[0, V:, :] = meta.astype(jnp.float32).astype(jnp.bfloat16)
    row = lax.broadcasted_iota(jnp.int32, (NF, V), 0)
    odd = jnp.zeros((NF, V), jnp.int32)
    for f in range(NF):
        odd = jnp.where(row == f, 2 * freq_ref[f] + 1, odd)
    odd_freq_ref[...] = odd.astype(jnp.float32)
    copies[0].wait()


def pack(freq_index, matrix, times, labels):
    vmem = pl.BlockSpec(memory_space=pltpu.VMEM)
    return pl.pallas_call(
        pack_kernel,
        out_shape=(
            jax.ShapeDtypeStruct((1, PACK, V), jnp.bfloat16),
            jax.ShapeDtypeStruct((NF, V), jnp.float32),
        ),
        in_specs=[pl.BlockSpec(memory_space=pl.ANY)] * 4,
        out_specs=(vmem, vmem),
        scratch_shapes=[
            pltpu.SMEM((NF,), jnp.int32),
            pltpu.VMEM((1, 1, V), jnp.int32),
            pltpu.VMEM((1, 1, V), jnp.int32),
            pltpu.SemaphoreType.DMA((4,)),
        ],
        compiler_params=pltpu.CompilerParams(vmem_limit_bytes=4 << 20),
        name="pack",
    )(*(pltpu.with_memory_space_constraint(x, pltpu.HBM) for x in (freq_index, matrix, times, labels)))


def absorb_kernel(first, share_ref, transfer_ref, odd_freq_ref, walkers_ref, *refs):
    if first:
        acc_ref, *slots = refs
        acc_ref[...] = jnp.zeros_like(acc_ref)
    else:
        old_ref, acc_ref, *slots = refs
    n = walkers_ref.shape[0]
    place = share_ref[0], transfer_ref[0], odd_freq_ref, walkers_ref
    slots = slots[0:2], slots[2:4]
    for piece in pieces(*place, 0, *slots[0]):
        piece()
    for w in range(n):
        todo = pieces(*place, w + 1, *slots[(w + 1) % 2]) if w + 1 < n else []
        for tile in range(4):
            tile_main(tile, *slots[w % 2], acc_ref)
            if tile < len(todo):
                todo[tile]()


def finish_kernel(share_ref, transfer_ref, odd_freq_ref, walkers_ref, old_ref, acc_ref, out_ref, *refs):
    n = walkers_ref.shape[0]
    place = share_ref[0], transfer_ref[0], odd_freq_ref, walkers_ref
    slots = [refs[2 * w : 2 * w + 2] for w in range(n)]
    sem = refs[2 * n]

    def copy(tile):
        cols = pl.ds(*COL_TILES[tile])
        return pltpu.make_async_copy(acc_ref.at[:, :, cols], out_ref.at[:, :, cols], sem.at[tile])

    for piece in pieces(*place, 0, *slots[0]):
        piece()
    for w in range(n):
        todo = pieces(*place, w + 1, *slots[w + 1]) if w + 1 < n else [lambda: None] * 3
        todo[0]()
        tile_main(0, *slots[w], acc_ref)
        todo[1]()
        if w + 1 == n:
            copy(0).start()
        tile_main(1, *slots[w], acc_ref)
        todo[2]()
    copy(1).start()
    for tile in (2, 3):
        for w in range(n):
            tile_main(tile, *slots[w], acc_ref)
        copy(tile).start()
    for tile in range(4):
        copy(tile).wait()


def absorb(share, transfer, odd_freq, walkers, acc=None, final=False):
    n = walkers.shape[0]
    vmem = pl.BlockSpec(memory_space=pltpu.VMEM)
    smem = pl.BlockSpec(memory_space=pltpu.SMEM)
    total = jax.ShapeDtypeStruct((2, ROWS, K), jnp.float32)
    args = [share, transfer, odd_freq, walkers] + ([] if acc is None else [acc])
    slots = n if final else 2
    result = pl.pallas_call(
        finish_kernel if final else lambda *refs: absorb_kernel(acc is None, *refs),
        out_shape=(total, total) if final else (total,),
        in_specs=[smem, smem] + [vmem] * (len(args) - 2),
        out_specs=(vmem, pl.BlockSpec(memory_space=pl.ANY)) if final else (vmem,),
        scratch_shapes=[pltpu.VMEM((K, 256), jnp.bfloat16)] * (2 * slots) + [pltpu.SemaphoreType.DMA((4,))] * final,
        input_output_aliases={} if acc is None else {4: 0},
        cost_estimate=pl.CostEstimate(flops=n * 450_000_000, bytes_accessed=n * 40_000, transcendentals=0),
        compiler_params=pltpu.CompilerParams(vmem_limit_bytes=16 << 20),
        name="finish" if final else "absorb",
    )(*args)
    return result[-1]


COORDS = ("x", "y", "zh", "zl", "core")


def permute(value, source):
    pairs = []
    for target in range(128):
        x, y, zh, zl, core = target // 32, target // 8 % 4, target // 4 % 2, target // 2 % 2, target % 2
        place = source(x, y, zh, zl, core)
        if place is not None:
            x, y, zh, zl, core = place
            pairs.append(((((x * 4 + y) * 2 + zh) * 2 + zl) * 2 + core, target))
    return lax.ppermute(value, COORDS, pairs)


def owner_at(steps):
    def source(x, y, zh, zl, core):
        owner = ((x * 4 + y) * 2 + zh + steps) % 32
        return owner // 8, owner // 2 % 4, owner % 2, zl, core

    return source


def after(value, *others):
    return lax.optimization_barrier((value, *others))


def local(walker_m, vertex_times, vertex_labels, freq_index, q_index):
    own, odd_freq = pack(freq_index, walker_m, vertex_times, vertex_labels)
    share = (2 * lax.axis_index("zl") + lax.axis_index("core")).astype(jnp.int32).reshape(1)

    def add(walkers, acc=None, final=False):
        return absorb(share, q_index, odd_freq, walkers, acc, final)

    behind = permute(own, owner_at(-2))
    ahead = permute(own, owner_at(2))
    acc = add(own)
    ahead, behind, acc = after(ahead, behind, acc)
    odd_owner = lax.axis_index("zh") == 1
    send = jnp.concatenate([own, jnp.where(odd_owner, behind, ahead)], axis=0)
    other = permute(send, lambda x, y, zh, zl, core: (x, y, 1 - zh, 1 - zl, core))
    acc = add(ahead, acc)
    other, acc = after(other, acc)
    group = jnp.concatenate([own, ahead, other], axis=0)
    near = permute(group, lambda x, y, zh, zl, core: (x, y, zh, 1 - zl, core))
    group_far = permute(group, lambda x, y, zh, zl, core: (x, y, zh, zl, 1 - core))
    acc = add(other, acc)
    group_far, acc = after(group_far, acc)
    acc = add(group_far, acc)
    near, acc = after(near, acc)
    near_far = permute(near, lambda x, y, zh, zl, core: (x, y, zh, zl, 1 - core))
    acc = add(near, acc)
    near_far, acc = after(near_far, acc)
    return add(near_far, acc, True)[None]


def solution(mesh):
    fine = Mesh(mesh.devices.reshape(4, 4, 2, 2, 2), COORDS)
    walk, blk = ("zl", "core"), ("x", "y", "zh")
    return jax.shard_map(
        local,
        mesh=fine,
        in_specs=(P(walk, blk, None, None), P(walk, blk, None), P(walk, blk, None), P(), P(blk)),
        out_specs=P(blk, None, walk, None),
        check_vma=False,
    )
```

```python
import jax
import jax.numpy as jnp
from jax import lax
from jax.experimental import pallas as pl
from jax.experimental.pallas import tpu as pltpu
from jax.sharding import Mesh
from jax.sharding import PartitionSpec as P

SIDE = 6
NF = 24
K = 864
V = 128
STEPS = 4
ROWS = 216
PACK = 136
BLOCKS = 9
COL_TILES = ((0, 256), (256, 256), (512, 256), (768, 96))


def quarter_cos_sin(turns):
    near = jnp.floor(turns + 0.5)
    x = turns - near
    x2 = x * x
    s = x * (1.5707963267948966 + x2 * (-0.6459640975062462 + x2 * (0.07969262624616704 + x2 * (-0.004681754135318688 + x2 * 0.00016044118478735982))))
    c = 1.0 + x2 * (-1.2337005501361697 + x2 * (0.253669507901048 + x2 * (-0.02086348076335296 + x2 * (0.0009192602748394266 + x2 * -2.520204237306061e-05))))
    quad = near - 4.0 * jnp.floor(near * 0.25)
    odd = (quad == 1.0) | (quad == 3.0)
    cc = jnp.where(odd, s, c)
    ss = jnp.where(odd, c, s)
    cc = jnp.where((quad == 1.0) | (quad == 2.0), -cc, cc)
    ss = jnp.where(quad >= 2.0, -ss, ss)
    return cc, ss


def sixth_cos_sin(m):
    y = m - 6.0 * jnp.floor((m + 0.5) * (1.0 / 6.0))
    z = jnp.abs(y - 3.0)
    half = 0.8660254037844386
    c = jnp.where(z == 3.0, 1.0, jnp.where(z == 2.0, 0.5, jnp.where(z == 1.0, -0.5, -1.0)))
    s = jnp.where((z == 3.0) | (z == 0.0), 0.0, jnp.where(y < 3.0, half, -half))
    return c, s


def pieces(share, transfer, odd_freq_ref, walkers_ref, w, table_ref, left_ref):
    st = {}

    def rotated(c, s, row):
        c, s = c[row : row + 1], s[row : row + 1]
        fc, fs = st["f"]
        return fc * c + fs * s, fs * c - fc * s

    def stacked(c, s):
        blocks = [rotated(c, s, j) for j in range(BLOCKS)]
        return jnp.concatenate([b[0] for b in blocks] + [b[1] for b in blocks], axis=0).astype(jnp.bfloat16)

    def interleave(parts):
        return jnp.stack([p.reshape(27, 8, V) for p in parts], axis=1).reshape(K, V).astype(jnp.bfloat16)

    def p0():
        meta = walkers_ref[w, V:, :].astype(jnp.float32)
        times = meta[0:1] * 32.0 + meta[1:2]
        sites = meta[2:3]
        site_x = jnp.floor((sites + 0.5) * (1.0 / SIDE))
        site_y = sites - SIDE * site_x
        product = odd_freq_ref[...] * times
        st["f"] = quarter_cos_sin((product - 2048.0 * jnp.floor(product * (1.0 / 2048.0))) * (1.0 / 512.0))

        def rows_of(kx, ky):
            return sixth_cos_sin(kx * site_x + ky * site_y)

        index = lax.broadcasted_iota(jnp.int32, (16, V), 0)
        st["base"] = rows_of((index // 3).astype(jnp.float32), (index % 3).astype(jnp.float32))
        mine = index + BLOCKS * share
        mine_x = (mine // SIDE).astype(jnp.float32)
        mine_y = (mine % SIDE).astype(jnp.float32)
        q_x = (transfer // SIDE).astype(jnp.float32)
        q_y = (transfer % SIDE).astype(jnp.float32)
        moved = rows_of(mine_x + q_x, mine_y + q_y)
        mine = rows_of(mine_x, mine_y)
        turn_c, turn_s = rows_of(q_x, q_y)
        st["turn"] = turn_c[0:1] * (2.0 ** -18), turn_s[0:1] * (2.0 ** -18)
        st["flip_x"] = 1.0 - 2.0 * (site_x - 2.0 * jnp.floor(site_x * 0.5))
        st["flip_y"] = 1.0 - 2.0 * (site_y - 2.0 * jnp.floor(site_y * 0.5))
        matrix = walkers_ref[w, :V, :]
        zero = jnp.zeros_like(matrix)
        weights = jnp.concatenate(
            [jnp.concatenate([matrix, zero], axis=1), jnp.concatenate([zero, matrix.T], axis=1)], axis=0
        )
        both = jnp.concatenate([stacked(*moved), stacked(*mine)], axis=1)
        both = jnp.dot(both, weights, preferred_element_type=jnp.float32)
        st["first"], st["second"] = both[:, 0:V], both[:, V:]

    def p1():
        base_c, base_s = st["base"]
        flip_x, flip_y = st["flip_x"], st["flip_y"]
        for kx in range(3):
            blocks = [rotated(base_c, base_s, 3 * kx + ky) for ky in range(3)]
            blocks = blocks + [(c * flip_y, s * flip_y) for c, s in blocks]
            cos_part = jnp.concatenate([b[0] for b in blocks], axis=0).astype(jnp.bfloat16)
            sin_part = jnp.concatenate([b[1] for b in blocks], axis=0).astype(jnp.bfloat16)
            flip = flip_x.astype(jnp.bfloat16)
            table_ref[pl.ds(144 * kx, 144), 0:V] = cos_part
            table_ref[pl.ds(144 * kx, 144), V:] = sin_part
            table_ref[pl.ds(144 * (kx + 3), 144), 0:V] = cos_part * flip
            table_ref[pl.ds(144 * (kx + 3), 144), V:] = sin_part * flip

    def p2():
        first = st["first"]
        a_re, a_im = first[:ROWS], first[ROWS:]
        turn_c, turn_s = st["turn"]
        st["a"] = a_re * turn_c - a_im * turn_s, a_re * turn_s + a_im * turn_c
        second = st["second"]
        a_re, a_im = st["a"]
        b_re, b_im = second[:ROWS], second[ROWS:]
        left_ref[:, 0:V] = interleave([a_re, a_im, b_re, -b_im])
        left_ref[:, V:] = interleave([a_im, -a_re, b_im, b_re])

    return [p0, p1, p2]


def tile_main(t, table_ref, left_ref, acc_ref):
    start, size = COL_TILES[t]
    cols = pl.ds(start, size)
    for chunk in range(3):
        product = lax.dot_general(
            left_ref[pl.ds(288 * chunk, 288), :],
            table_ref[cols, :],
            (((1,), (1,)), ((), ())),
            preferred_element_type=jnp.float32,
        ).reshape(9, 4, 8, size)
        m_re, m_im, n_re, n_im = (product[:, i] for i in range(4))
        rows = pl.ds(72 * chunk, 72)
        acc_ref[0, rows, cols] += (m_re * n_re - m_im * n_im).reshape(72, size)
        acc_ref[1, rows, cols] += (m_re * n_im + m_im * n_re).reshape(72, size)


def pack_kernel(freq_hbm, matrix_hbm, times_hbm, labels_hbm, packed_ref, odd_freq_ref, freq_ref, times_ref, labels_ref, sem):
    copies = (
        pltpu.make_async_copy(matrix_hbm.at[0], packed_ref.at[:, pl.ds(0, V), :], sem.at[0]),
        pltpu.make_async_copy(times_hbm, times_ref, sem.at[1]),
        pltpu.make_async_copy(labels_hbm, labels_ref, sem.at[2]),
        pltpu.make_async_copy(freq_hbm, freq_ref, sem.at[3]),
    )
    for copy in copies:
        copy.start()
    for copy in copies[1:]:
        copy.wait()
    row = lax.broadcasted_iota(jnp.int32, (PACK - V, V), 0)
    times = jnp.broadcast_to(times_ref[0], (PACK - V, V))
    labels = jnp.broadcast_to(labels_ref[0], (PACK - V, V))
    meta = jnp.where(row == 0, times // 32, jnp.where(row == 1, times % 32, jnp.where(row == 2, labels, 0)))
    packed_ref[0, V:, :] = meta.astype(jnp.float32).astype(jnp.bfloat16)
    row = lax.broadcasted_iota(jnp.int32, (NF, V), 0)
    odd = jnp.zeros((NF, V), jnp.int32)
    for f in range(NF):
        odd = jnp.where(row == f, 2 * freq_ref[f] + 1, odd)
    odd_freq_ref[...] = odd.astype(jnp.float32)
    copies[0].wait()


def pack(freq_index, matrix, times, labels):
    vmem = pl.BlockSpec(memory_space=pltpu.VMEM)
    return pl.pallas_call(
        pack_kernel,
        out_shape=(
            jax.ShapeDtypeStruct((1, PACK, V), jnp.bfloat16),
            jax.ShapeDtypeStruct((NF, V), jnp.float32),
        ),
        in_specs=[pl.BlockSpec(memory_space=pl.ANY)] * 4,
        out_specs=(vmem, vmem),
        scratch_shapes=[
            pltpu.SMEM((NF,), jnp.int32),
            pltpu.VMEM((1, 1, V), jnp.int32),
            pltpu.VMEM((1, 1, V), jnp.int32),
            pltpu.SemaphoreType.DMA((4,)),
        ],
        compiler_params=pltpu.CompilerParams(vmem_limit_bytes=4 << 20),
        name="pack",
    )(*(pltpu.with_memory_space_constraint(x, pltpu.HBM) for x in (freq_index, matrix, times, labels)))


def absorb_kernel(first, share_ref, transfer_ref, odd_freq_ref, walkers_ref, *refs):
    if first:
        acc_ref, *slots = refs
        acc_ref[...] = jnp.zeros_like(acc_ref)
    else:
        old_ref, acc_ref, *slots = refs
    n = walkers_ref.shape[0]
    place = share_ref[0], transfer_ref[0], odd_freq_ref, walkers_ref
    slots = slots[0:2], slots[2:4]
    for piece in pieces(*place, 0, *slots[0]):
        piece()
    for w in range(n):
        todo = pieces(*place, w + 1, *slots[(w + 1) % 2]) if w + 1 < n else []
        for tile in range(4):
            tile_main(tile, *slots[w % 2], acc_ref)
            if tile < len(todo):
                todo[tile]()


def finish_kernel(share_ref, transfer_ref, odd_freq_ref, walkers_ref, old_ref, acc_ref, out_ref, *refs):
    n = walkers_ref.shape[0]
    place = share_ref[0], transfer_ref[0], odd_freq_ref, walkers_ref
    slots = [refs[2 * w : 2 * w + 2] for w in range(n)]
    sem = refs[2 * n]

    def copy(tile):
        cols = pl.ds(*COL_TILES[tile])
        return pltpu.make_async_copy(acc_ref.at[:, :, cols], out_ref.at[:, :, cols], sem.at[tile])

    for piece in pieces(*place, 0, *slots[0]):
        piece()
    for w in range(n):
        todo = pieces(*place, w + 1, *slots[w + 1]) if w + 1 < n else [lambda: None] * 3
        todo[0]()
        tile_main(0, *slots[w], acc_ref)
        todo[1]()
        if w + 1 == n:
            copy(0).start()
        tile_main(1, *slots[w], acc_ref)
        todo[2]()
    copy(1).start()
    for tile in (2, 3):
        for w in range(n):
            tile_main(tile, *slots[w], acc_ref)
        copy(tile).start()
    for tile in range(4):
        copy(tile).wait()


def absorb(share, transfer, odd_freq, walkers, acc=None, final=False):
    n = walkers.shape[0]
    vmem = pl.BlockSpec(memory_space=pltpu.VMEM)
    smem = pl.BlockSpec(memory_space=pltpu.SMEM)
    total = jax.ShapeDtypeStruct((2, ROWS, K), jnp.float32)
    args = [share, transfer, odd_freq, walkers] + ([] if acc is None else [acc])
    slots = n if final else 2
    result = pl.pallas_call(
        finish_kernel if final else lambda *refs: absorb_kernel(acc is None, *refs),
        out_shape=(total, total) if final else (total,),
        in_specs=[smem, smem] + [vmem] * (len(args) - 2),
        out_specs=(vmem, pl.BlockSpec(memory_space=pl.ANY)) if final else (vmem,),
        scratch_shapes=[pltpu.VMEM((K, 256), jnp.bfloat16)] * (2 * slots) + [pltpu.SemaphoreType.DMA((4,))] * final,
        input_output_aliases={} if acc is None else {4: 0},
        cost_estimate=pl.CostEstimate(flops=n * 450_000_000, bytes_accessed=n * 40_000, transcendentals=0),
        compiler_params=pltpu.CompilerParams(vmem_limit_bytes=16 << 20),
        name="finish" if final else "absorb",
    )(*args)
    return result[-1]


COORDS = ("x", "y", "zh", "zl", "core")


def permute(value, source):
    pairs = []
    for target in range(128):
        x, y, zh, zl, core = target // 32, target // 8 % 4, target // 4 % 2, target // 2 % 2, target % 2
        place = source(x, y, zh, zl, core)
        if place is not None:
            x, y, zh, zl, core = place
            pairs.append(((((x * 4 + y) * 2 + zh) * 2 + zl) * 2 + core, target))
    return lax.ppermute(value, COORDS, pairs)


def owner_at(steps):
    def source(x, y, zh, zl, core):
        owner = ((x * 4 + y) * 2 + zh + steps) % 32
        return owner // 8, owner // 2 % 4, owner % 2, zl, core

    return source


def after(value, *others):
    return lax.optimization_barrier((value, *others))


def local(walker_m, vertex_times, vertex_labels, freq_index, q_index):
    own, odd_freq = pack(freq_index, walker_m, vertex_times, vertex_labels)
    share = (2 * lax.axis_index("zl") + lax.axis_index("core")).astype(jnp.int32).reshape(1)

    def add(walkers, acc=None, final=False):
        return absorb(share, q_index, odd_freq, walkers, acc, final)

    behind = permute(own, owner_at(-2))
    ahead = permute(own, owner_at(2))
    acc = add(own)
    ahead, behind, acc = after(ahead, behind, acc)
    odd_owner = lax.axis_index("zh") == 1
    send = jnp.concatenate([own, jnp.where(odd_owner, behind, ahead)], axis=0)
    other = permute(send, lambda x, y, zh, zl, core: (x, y, 1 - zh, 1 - zl, core))
    acc = add(ahead, acc)
    other, acc = after(other, acc)
    group = jnp.concatenate([own, ahead, other], axis=0)
    near = permute(group, lambda x, y, zh, zl, core: (x, y, zh, 1 - zl, core))
    group_far = permute(group, lambda x, y, zh, zl, core: (x, y, zh, zl, 1 - core))
    acc = add(other, acc)
    group_far, acc = after(group_far, acc)
    acc = add(group_far, acc)
    near, acc = after(near, acc)
    near_far = permute(near, lambda x, y, zh, zl, core: (x, y, zh, zl, 1 - core))
    acc = add(near, acc)
    near_far, acc = after(near_far, acc)
    return add(near_far, acc, True)[None]


def solution(mesh):
    fine = Mesh(mesh.devices.reshape(4, 4, 2, 2, 2), COORDS)
    walk, blk = ("zl", "core"), ("x", "y", "zh")
    return jax.shard_map(
        local,
        mesh=fine,
        in_specs=(P(walk, blk, None, None), P(walk, blk, None), P(walk, blk, None), P(), P(blk)),
        out_specs=P(blk, None, walk, None),
        check_vma=False,
    )
```

```python
import jax
import jax.numpy as jnp
from jax import lax
from jax.experimental import pallas as pl
from jax.experimental.pallas import tpu as pltpu
from jax.sharding import Mesh
from jax.sharding import PartitionSpec as P

SIDE = 6
NF = 24
K = 864
V = 128
STEPS = 4
ROWS = 216
PACK = 136
BLOCKS = 9
COL_TILES = ((0, 256), (256, 256), (512, 256), (768, 96))


def quarter_cos_sin(turns):
    near = jnp.floor(turns + 0.5)
    x = turns - near
    x2 = x * x
    s = x * (1.5707963267948966 + x2 * (-0.6459640975062462 + x2 * (0.07969262624616704 + x2 * (-0.004681754135318688 + x2 * 0.00016044118478735982))))
    c = 1.0 + x2 * (-1.2337005501361697 + x2 * (0.253669507901048 + x2 * (-0.02086348076335296 + x2 * (0.0009192602748394266 + x2 * -2.520204237306061e-05))))
    quad = near - 4.0 * jnp.floor(near * 0.25)
    odd = (quad == 1.0) | (quad == 3.0)
    cc = jnp.where(odd, s, c)
    ss = jnp.where(odd, c, s)
    cc = jnp.where((quad == 1.0) | (quad == 2.0), -cc, cc)
    ss = jnp.where(quad >= 2.0, -ss, ss)
    return cc, ss


def sixth_cos_sin(m):
    y = m - 6.0 * jnp.floor((m + 0.5) * (1.0 / 6.0))
    z = jnp.abs(y - 3.0)
    half = 0.8660254037844386
    c = jnp.where(z == 3.0, 1.0, jnp.where(z == 2.0, 0.5, jnp.where(z == 1.0, -0.5, -1.0)))
    s = jnp.where((z == 3.0) | (z == 0.0), 0.0, jnp.where(y < 3.0, half, -half))
    return c, s


def pieces(share, transfer, odd_freq_ref, walkers_ref, w, table_ref, left_ref):
    st = {}

    def rotated(c, s, row):
        c, s = c[row : row + 1], s[row : row + 1]
        fc, fs = st["f"]
        return fc * c + fs * s, fs * c - fc * s

    def stacked(c, s):
        blocks = [rotated(c, s, j) for j in range(BLOCKS)]
        return jnp.concatenate([b[0] for b in blocks] + [b[1] for b in blocks], axis=0).astype(jnp.bfloat16)

    def interleave(parts):
        return jnp.stack([p.reshape(27, 8, V) for p in parts], axis=1).reshape(K, V).astype(jnp.bfloat16)

    def p0():
        meta = walkers_ref[w, V:, :].astype(jnp.float32)
        times = meta[0:1] * 32.0 + meta[1:2]
        sites = meta[2:3]
        site_x = jnp.floor((sites + 0.5) * (1.0 / SIDE))
        site_y = sites - SIDE * site_x
        product = odd_freq_ref[...] * times
        st["f"] = quarter_cos_sin((product - 2048.0 * jnp.floor(product * (1.0 / 2048.0))) * (1.0 / 512.0))

        def rows_of(kx, ky):
            return sixth_cos_sin(kx * site_x + ky * site_y)

        index = lax.broadcasted_iota(jnp.int32, (16, V), 0)
        st["base"] = rows_of((index // 3).astype(jnp.float32), (index % 3).astype(jnp.float32))
        mine = index + BLOCKS * share
        mine_x = (mine // SIDE).astype(jnp.float32)
        mine_y = (mine % SIDE).astype(jnp.float32)
        q_x = (transfer // SIDE).astype(jnp.float32)
        q_y = (transfer % SIDE).astype(jnp.float32)
        moved = rows_of(mine_x + q_x, mine_y + q_y)
        mine = rows_of(mine_x, mine_y)
        turn_c, turn_s = rows_of(q_x, q_y)
        st["turn"] = turn_c[0:1] * (2.0 ** -18), turn_s[0:1] * (2.0 ** -18)
        st["flip_x"] = 1.0 - 2.0 * (site_x - 2.0 * jnp.floor(site_x * 0.5))
        st["flip_y"] = 1.0 - 2.0 * (site_y - 2.0 * jnp.floor(site_y * 0.5))
        matrix = walkers_ref[w, :V, :]
        zero = jnp.zeros_like(matrix)
        weights = jnp.concatenate(
            [jnp.concatenate([matrix, zero], axis=1), jnp.concatenate([zero, matrix.T], axis=1)], axis=0
        )
        both = jnp.concatenate([stacked(*moved), stacked(*mine)], axis=1)
        both = jnp.dot(both, weights, preferred_element_type=jnp.float32)
        st["first"], st["second"] = both[:, 0:V], both[:, V:]

    def p1():
        base_c, base_s = st["base"]
        flip_x, flip_y = st["flip_x"], st["flip_y"]
        for kx in range(3):
            blocks = [rotated(base_c, base_s, 3 * kx + ky) for ky in range(3)]
            blocks = blocks + [(c * flip_y, s * flip_y) for c, s in blocks]
            cos_part = jnp.concatenate([b[0] for b in blocks], axis=0).astype(jnp.bfloat16)
            sin_part = jnp.concatenate([b[1] for b in blocks], axis=0).astype(jnp.bfloat16)
            flip = flip_x.astype(jnp.bfloat16)
            table_ref[pl.ds(144 * kx, 144), 0:V] = cos_part
            table_ref[pl.ds(144 * kx, 144), V:] = sin_part
            table_ref[pl.ds(144 * (kx + 3), 144), 0:V] = cos_part * flip
            table_ref[pl.ds(144 * (kx + 3), 144), V:] = sin_part * flip

    def p2():
        first = st["first"]
        a_re, a_im = first[:ROWS], first[ROWS:]
        turn_c, turn_s = st["turn"]
        st["a"] = a_re * turn_c - a_im * turn_s, a_re * turn_s + a_im * turn_c
        second = st["second"]
        a_re, a_im = st["a"]
        b_re, b_im = second[:ROWS], second[ROWS:]
        left_ref[:, 0:V] = interleave([a_re, a_im, b_re, -b_im])
        left_ref[:, V:] = interleave([a_im, -a_re, b_im, b_re])

    return [p0, p1, p2]


def tile_main(t, table_ref, left_ref, acc_ref):
    start, size = COL_TILES[t]
    cols = pl.ds(start, size)
    for chunk in range(3):
        product = lax.dot_general(
            left_ref[pl.ds(288 * chunk, 288), :],
            table_ref[cols, :],
            (((1,), (1,)), ((), ())),
            preferred_element_type=jnp.float32,
        ).reshape(9, 4, 8, size)
        m_re, m_im, n_re, n_im = (product[:, i] for i in range(4))
        rows = pl.ds(72 * chunk, 72)
        acc_ref[0, rows, cols] += (m_re * n_re - m_im * n_im).reshape(72, size)
        acc_ref[1, rows, cols] += (m_re * n_im + m_im * n_re).reshape(72, size)


def pack_kernel(freq_hbm, matrix_hbm, times_hbm, labels_hbm, packed_ref, odd_freq_ref, freq_ref, times_ref, labels_ref, sem):
    copies = (
        pltpu.make_async_copy(matrix_hbm.at[0], packed_ref.at[:, pl.ds(0, V), :], sem.at[0]),
        pltpu.make_async_copy(times_hbm, times_ref, sem.at[1]),
        pltpu.make_async_copy(labels_hbm, labels_ref, sem.at[2]),
        pltpu.make_async_copy(freq_hbm, freq_ref, sem.at[3]),
    )
    for copy in copies:
        copy.start()
    for copy in copies[1:]:
        copy.wait()
    row = lax.broadcasted_iota(jnp.int32, (PACK - V, V), 0)
    times = jnp.broadcast_to(times_ref[0], (PACK - V, V))
    labels = jnp.broadcast_to(labels_ref[0], (PACK - V, V))
    meta = jnp.where(row == 0, times // 32, jnp.where(row == 1, times % 32, jnp.where(row == 2, labels, 0)))
    packed_ref[0, V:, :] = meta.astype(jnp.float32).astype(jnp.bfloat16)
    row = lax.broadcasted_iota(jnp.int32, (NF, V), 0)
    odd = jnp.zeros((NF, V), jnp.int32)
    for f in range(NF):
        odd = jnp.where(row == f, 2 * freq_ref[f] + 1, odd)
    odd_freq_ref[...] = odd.astype(jnp.float32)
    copies[0].wait()


def pack(freq_index, matrix, times, labels):
    vmem = pl.BlockSpec(memory_space=pltpu.VMEM)
    return pl.pallas_call(
        pack_kernel,
        out_shape=(
            jax.ShapeDtypeStruct((1, PACK, V), jnp.bfloat16),
            jax.ShapeDtypeStruct((NF, V), jnp.float32),
        ),
        in_specs=[pl.BlockSpec(memory_space=pl.ANY)] * 4,
        out_specs=(vmem, vmem),
        scratch_shapes=[
            pltpu.SMEM((NF,), jnp.int32),
            pltpu.VMEM((1, 1, V), jnp.int32),
            pltpu.VMEM((1, 1, V), jnp.int32),
            pltpu.SemaphoreType.DMA((4,)),
        ],
        compiler_params=pltpu.CompilerParams(vmem_limit_bytes=4 << 20),
        name="pack",
    )(*(pltpu.with_memory_space_constraint(x, pltpu.HBM) for x in (freq_index, matrix, times, labels)))


def absorb_kernel(first, share_ref, transfer_ref, odd_freq_ref, walkers_ref, *refs):
    if first:
        acc_ref, *slots = refs
        acc_ref[...] = jnp.zeros_like(acc_ref)
    else:
        old_ref, acc_ref, *slots = refs
    n = walkers_ref.shape[0]
    place = share_ref[0], transfer_ref[0], odd_freq_ref, walkers_ref
    slots = slots[0:2], slots[2:4]
    for piece in pieces(*place, 0, *slots[0]):
        piece()
    for w in range(n):
        todo = pieces(*place, w + 1, *slots[(w + 1) % 2]) if w + 1 < n else []
        for tile in range(4):
            tile_main(tile, *slots[w % 2], acc_ref)
            if tile < len(todo):
                todo[tile]()


def finish_kernel(share_ref, transfer_ref, odd_freq_ref, walkers_ref, old_ref, acc_ref, out_ref, *refs):
    n = walkers_ref.shape[0]
    place = share_ref[0], transfer_ref[0], odd_freq_ref, walkers_ref
    slots = [refs[2 * w : 2 * w + 2] for w in range(n)]
    sem = refs[2 * n]

    def copy(tile):
        cols = pl.ds(*COL_TILES[tile])
        return pltpu.make_async_copy(acc_ref.at[:, :, cols], out_ref.at[:, :, cols], sem.at[tile])

    for piece in pieces(*place, 0, *slots[0]):
        piece()
    for w in range(n):
        todo = pieces(*place, w + 1, *slots[w + 1]) if w + 1 < n else [lambda: None] * 3
        todo[0]()
        tile_main(0, *slots[w], acc_ref)
        todo[1]()
        if w + 1 == n:
            copy(0).start()
        tile_main(1, *slots[w], acc_ref)
        todo[2]()
    copy(1).start()
    for tile in (2, 3):
        for w in range(n):
            tile_main(tile, *slots[w], acc_ref)
        copy(tile).start()
    for tile in range(4):
        copy(tile).wait()


def absorb(share, transfer, odd_freq, walkers, acc=None, final=False):
    n = walkers.shape[0]
    vmem = pl.BlockSpec(memory_space=pltpu.VMEM)
    smem = pl.BlockSpec(memory_space=pltpu.SMEM)
    total = jax.ShapeDtypeStruct((2, ROWS, K), jnp.float32)
    args = [share, transfer, odd_freq, walkers] + ([] if acc is None else [acc])
    slots = n if final else 2
    result = pl.pallas_call(
        finish_kernel if final else lambda *refs: absorb_kernel(acc is None, *refs),
        out_shape=(total, total) if final else (total,),
        in_specs=[smem, smem] + [vmem] * (len(args) - 2),
        out_specs=(vmem, pl.BlockSpec(memory_space=pl.ANY)) if final else (vmem,),
        scratch_shapes=[pltpu.VMEM((K, 256), jnp.bfloat16)] * (2 * slots) + [pltpu.SemaphoreType.DMA((4,))] * final,
        input_output_aliases={} if acc is None else {4: 0},
        cost_estimate=pl.CostEstimate(flops=n * 450_000_000, bytes_accessed=n * 40_000, transcendentals=0),
        compiler_params=pltpu.CompilerParams(vmem_limit_bytes=16 << 20),
        name="finish" if final else "absorb",
    )(*args)
    return result[-1]


COORDS = ("x", "y", "zh", "zl", "core")


def permute(value, source):
    pairs = []
    for target in range(128):
        x, y, zh, zl, core = target // 32, target // 8 % 4, target // 4 % 2, target // 2 % 2, target % 2
        place = source(x, y, zh, zl, core)
        if place is not None:
            x, y, zh, zl, core = place
            pairs.append(((((x * 4 + y) * 2 + zh) * 2 + zl) * 2 + core, target))
    return lax.ppermute(value, COORDS, pairs)


def owner_at(steps):
    def source(x, y, zh, zl, core):
        owner = ((x * 4 + y) * 2 + zh + steps) % 32
        return owner // 8, owner // 2 % 4, owner % 2, zl, core

    return source


def after(value, *others):
    return lax.optimization_barrier((value, *others))


def local(walker_m, vertex_times, vertex_labels, freq_index, q_index):
    own, odd_freq = pack(freq_index, walker_m, vertex_times, vertex_labels)
    share = (2 * lax.axis_index("zl") + lax.axis_index("core")).astype(jnp.int32).reshape(1)

    def add(walkers, acc=None, final=False):
        return absorb(share, q_index, odd_freq, walkers, acc, final)

    def flip_zl(x, y, zh, zl, core):
        return x, y, zh, 1 - zl, core

    def flip_core(x, y, zh, zl, core):
        return x, y, zh, zl, 1 - core

    def flip_z(x, y, zh, zl, core):
        return x, y, 1 - zh, 1 - zl, core

    behind = permute(own, owner_at(-2))
    ahead = permute(own, owner_at(2))
    early = permute(own, flip_zl)
    acc = add(own)
    ahead, behind, early, acc = after(ahead, behind, early, acc)
    odd_owner = lax.axis_index("zh") == 1
    send = jnp.concatenate([own, jnp.where(odd_owner, behind, ahead)], axis=0)
    other = permute(send, flip_z)
    acc = add(jnp.concatenate([early, ahead], axis=0), acc)
    other, acc = after(other, acc)
    group = jnp.concatenate([own, ahead, other, early], axis=0)
    near = permute(group[1:4], flip_zl)
    group_far = permute(group, flip_core)
    acc = add(other, acc)
    group_far, acc = after(group_far, acc)
    acc = add(group_far, acc)
    near, acc = after(near, acc)
    near_far = permute(near, flip_core)
    acc = add(near, acc)
    near_far, acc = after(near_far, acc)
    return add(near_far, acc, True)[None]


def solution(mesh):
    fine = Mesh(mesh.devices.reshape(4, 4, 2, 2, 2), COORDS)
    walk, blk = ("zl", "core"), ("x", "y", "zh")
    return jax.shard_map(
        local,
        mesh=fine,
        in_specs=(P(walk, blk, None, None), P(walk, blk, None), P(walk, blk, None), P(), P(blk)),
        out_specs=P(blk, None, walk, None),
        check_vma=False,
    )
```

```python
import jax
import jax.numpy as jnp
from jax import lax
from jax.experimental import pallas as pl
from jax.experimental.pallas import tpu as pltpu
from jax.sharding import Mesh
from jax.sharding import PartitionSpec as P

SIDE = 6
NF = 24
K = 864
V = 128
STEPS = 4
ROWS = 216
PACK = 136
BLOCKS = 9
COL_TILES = ((0, 256), (256, 256), (512, 256), (768, 96))


def quarter_cos_sin(turns):
    near = jnp.floor(turns + 0.5)
    x = turns - near
    x2 = x * x
    s = x * (1.5707963267948966 + x2 * (-0.6459640975062462 + x2 * (0.07969262624616704 + x2 * (-0.004681754135318688 + x2 * 0.00016044118478735982))))
    c = 1.0 + x2 * (-1.2337005501361697 + x2 * (0.253669507901048 + x2 * (-0.02086348076335296 + x2 * (0.0009192602748394266 + x2 * -2.520204237306061e-05))))
    quad = near - 4.0 * jnp.floor(near * 0.25)
    odd = (quad == 1.0) | (quad == 3.0)
    cc = jnp.where(odd, s, c)
    ss = jnp.where(odd, c, s)
    cc = jnp.where((quad == 1.0) | (quad == 2.0), -cc, cc)
    ss = jnp.where(quad >= 2.0, -ss, ss)
    return cc, ss


def sixth_cos_sin(m):
    y = m - 6.0 * jnp.floor((m + 0.5) * (1.0 / 6.0))
    z = jnp.abs(y - 3.0)
    half = 0.8660254037844386
    c = jnp.where(z == 3.0, 1.0, jnp.where(z == 2.0, 0.5, jnp.where(z == 1.0, -0.5, -1.0)))
    s = jnp.where((z == 3.0) | (z == 0.0), 0.0, jnp.where(y < 3.0, half, -half))
    return c, s


def pieces(share, transfer, odd_freq_ref, walkers_ref, w, table_ref, left_ref):
    st = {}

    def rotated(c, s, row):
        c, s = c[row : row + 1], s[row : row + 1]
        fc, fs = st["f"]
        return fc * c + fs * s, fs * c - fc * s

    def stacked(c, s):
        blocks = [rotated(c, s, j) for j in range(BLOCKS)]
        return jnp.concatenate([b[0] for b in blocks] + [b[1] for b in blocks], axis=0).astype(jnp.bfloat16)

    def interleave(parts):
        return jnp.stack([p.reshape(27, 8, V) for p in parts], axis=1).reshape(K, V).astype(jnp.bfloat16)

    def p0():
        meta = walkers_ref[w, V:, :].astype(jnp.float32)
        times = meta[0:1] * 32.0 + meta[1:2]
        sites = meta[2:3]
        site_x = jnp.floor((sites + 0.5) * (1.0 / SIDE))
        site_y = sites - SIDE * site_x
        product = odd_freq_ref[...] * times
        st["f"] = quarter_cos_sin((product - 2048.0 * jnp.floor(product * (1.0 / 2048.0))) * (1.0 / 512.0))

        def rows_of(kx, ky):
            return sixth_cos_sin(kx * site_x + ky * site_y)

        index = lax.broadcasted_iota(jnp.int32, (16, V), 0)
        st["base"] = rows_of((index // 3).astype(jnp.float32), (index % 3).astype(jnp.float32))
        mine = index + BLOCKS * share
        mine_x = (mine // SIDE).astype(jnp.float32)
        mine_y = (mine % SIDE).astype(jnp.float32)
        q_x = (transfer // SIDE).astype(jnp.float32)
        q_y = (transfer % SIDE).astype(jnp.float32)
        moved = rows_of(mine_x + q_x, mine_y + q_y)
        mine = rows_of(mine_x, mine_y)
        turn_c, turn_s = rows_of(q_x, q_y)
        st["turn"] = turn_c[0:1] * (2.0 ** -18), turn_s[0:1] * (2.0 ** -18)
        st["flip_x"] = 1.0 - 2.0 * (site_x - 2.0 * jnp.floor(site_x * 0.5))
        st["flip_y"] = 1.0 - 2.0 * (site_y - 2.0 * jnp.floor(site_y * 0.5))
        matrix = walkers_ref[w, :V, :]
        zero = jnp.zeros_like(matrix)
        weights = jnp.concatenate(
            [jnp.concatenate([matrix, zero], axis=1), jnp.concatenate([zero, matrix.T], axis=1)], axis=0
        )
        both = jnp.concatenate([stacked(*moved), stacked(*mine)], axis=1)
        both = jnp.dot(both, weights, preferred_element_type=jnp.float32)
        st["first"], st["second"] = both[:, 0:V], both[:, V:]

    def p1():
        base_c, base_s = st["base"]
        flip_x, flip_y = st["flip_x"], st["flip_y"]
        for kx in range(3):
            blocks = [rotated(base_c, base_s, 3 * kx + ky) for ky in range(3)]
            blocks = blocks + [(c * flip_y, s * flip_y) for c, s in blocks]
            cos_part = jnp.concatenate([b[0] for b in blocks], axis=0).astype(jnp.bfloat16)
            sin_part = jnp.concatenate([b[1] for b in blocks], axis=0).astype(jnp.bfloat16)
            flip = flip_x.astype(jnp.bfloat16)
            table_ref[pl.ds(144 * kx, 144), 0:V] = cos_part
            table_ref[pl.ds(144 * kx, 144), V:] = sin_part
            table_ref[pl.ds(144 * (kx + 3), 144), 0:V] = cos_part * flip
            table_ref[pl.ds(144 * (kx + 3), 144), V:] = sin_part * flip

    def p2():
        first = st["first"]
        a_re, a_im = first[:ROWS], first[ROWS:]
        turn_c, turn_s = st["turn"]
        st["a"] = a_re * turn_c - a_im * turn_s, a_re * turn_s + a_im * turn_c
        second = st["second"]
        a_re, a_im = st["a"]
        b_re, b_im = second[:ROWS], second[ROWS:]
        left_ref[:, 0:V] = interleave([a_re, a_im, b_re, -b_im])
        left_ref[:, V:] = interleave([a_im, -a_re, b_im, b_re])

    return [p0, p1, p2]


def tile_main(t, table_ref, left_ref, acc_ref):
    start, size = COL_TILES[t]
    cols = pl.ds(start, size)
    for chunk in range(3):
        product = lax.dot_general(
            left_ref[pl.ds(288 * chunk, 288), :],
            table_ref[cols, :],
            (((1,), (1,)), ((), ())),
            preferred_element_type=jnp.float32,
        ).reshape(9, 4, 8, size)
        m_re, m_im, n_re, n_im = (product[:, i] for i in range(4))
        rows = pl.ds(72 * chunk, 72)
        acc_ref[0, rows, cols] += (m_re * n_re - m_im * n_im).reshape(72, size)
        acc_ref[1, rows, cols] += (m_re * n_im + m_im * n_re).reshape(72, size)


def pack_kernel(freq_hbm, matrix_hbm, times_hbm, labels_hbm, packed_ref, odd_freq_ref, freq_ref, times_ref, labels_ref, sem):
    copies = (
        pltpu.make_async_copy(matrix_hbm.at[0], packed_ref.at[:, pl.ds(0, V), :], sem.at[0]),
        pltpu.make_async_copy(times_hbm, times_ref, sem.at[1]),
        pltpu.make_async_copy(labels_hbm, labels_ref, sem.at[2]),
        pltpu.make_async_copy(freq_hbm, freq_ref, sem.at[3]),
    )
    for copy in copies:
        copy.start()
    for copy in copies[1:]:
        copy.wait()
    row = lax.broadcasted_iota(jnp.int32, (PACK - V, V), 0)
    times = jnp.broadcast_to(times_ref[0], (PACK - V, V))
    labels = jnp.broadcast_to(labels_ref[0], (PACK - V, V))
    meta = jnp.where(row == 0, times // 32, jnp.where(row == 1, times % 32, jnp.where(row == 2, labels, 0)))
    packed_ref[0, V:, :] = meta.astype(jnp.float32).astype(jnp.bfloat16)
    row = lax.broadcasted_iota(jnp.int32, (NF, V), 0)
    odd = jnp.zeros((NF, V), jnp.int32)
    for f in range(NF):
        odd = jnp.where(row == f, 2 * freq_ref[f] + 1, odd)
    odd_freq_ref[...] = odd.astype(jnp.float32)
    copies[0].wait()


def pack(freq_index, matrix, times, labels):
    vmem = pl.BlockSpec(memory_space=pltpu.VMEM)
    return pl.pallas_call(
        pack_kernel,
        out_shape=(
            jax.ShapeDtypeStruct((1, PACK, V), jnp.bfloat16),
            jax.ShapeDtypeStruct((NF, V), jnp.float32),
        ),
        in_specs=[pl.BlockSpec(memory_space=pl.ANY)] * 4,
        out_specs=(vmem, vmem),
        scratch_shapes=[
            pltpu.SMEM((NF,), jnp.int32),
            pltpu.VMEM((1, 1, V), jnp.int32),
            pltpu.VMEM((1, 1, V), jnp.int32),
            pltpu.SemaphoreType.DMA((4,)),
        ],
        compiler_params=pltpu.CompilerParams(vmem_limit_bytes=4 << 20),
        name="pack",
    )(*(pltpu.with_memory_space_constraint(x, pltpu.HBM) for x in (freq_index, matrix, times, labels)))


def absorb_kernel(first, share_ref, transfer_ref, odd_freq_ref, walkers_ref, *refs):
    if first:
        acc_ref, *slots = refs
        acc_ref[...] = jnp.zeros_like(acc_ref)
    else:
        old_ref, acc_ref, *slots = refs
    n = walkers_ref.shape[0]
    place = share_ref[0], transfer_ref[0], odd_freq_ref, walkers_ref
    slots = slots[0:2], slots[2:4]
    for piece in pieces(*place, 0, *slots[0]):
        piece()
    for w in range(n):
        todo = pieces(*place, w + 1, *slots[(w + 1) % 2]) if w + 1 < n else []
        for tile in range(4):
            tile_main(tile, *slots[w % 2], acc_ref)
            if tile < len(todo):
                todo[tile]()


def finish_kernel(share_ref, transfer_ref, odd_freq_ref, walkers_ref, old_ref, acc_ref, out_ref, *refs):
    n = walkers_ref.shape[0]
    place = share_ref[0], transfer_ref[0], odd_freq_ref, walkers_ref
    slots = [refs[2 * w : 2 * w + 2] for w in range(n)]
    sem = refs[2 * n]

    def copy(tile):
        cols = pl.ds(*COL_TILES[tile])
        return pltpu.make_async_copy(acc_ref.at[:, :, cols], out_ref.at[:, :, cols], sem.at[tile])

    for piece in pieces(*place, 0, *slots[0]):
        piece()
    for w in range(n):
        todo = pieces(*place, w + 1, *slots[w + 1]) if w + 1 < n else [lambda: None] * 3
        todo[0]()
        tile_main(0, *slots[w], acc_ref)
        todo[1]()
        if w + 1 == n:
            copy(0).start()
        tile_main(1, *slots[w], acc_ref)
        todo[2]()
    copy(1).start()
    for tile in (2, 3):
        for w in range(n):
            tile_main(tile, *slots[w], acc_ref)
        copy(tile).start()
    for tile in range(4):
        copy(tile).wait()


def absorb(share, transfer, odd_freq, walkers, acc=None, final=False):
    n = walkers.shape[0]
    vmem = pl.BlockSpec(memory_space=pltpu.VMEM)
    smem = pl.BlockSpec(memory_space=pltpu.SMEM)
    total = jax.ShapeDtypeStruct((2, ROWS, K), jnp.float32)
    args = [share, transfer, odd_freq, walkers] + ([] if acc is None else [acc])
    slots = n if final else 2
    result = pl.pallas_call(
        finish_kernel if final else lambda *refs: absorb_kernel(acc is None, *refs),
        out_shape=(total, total) if final else (total,),
        in_specs=[smem, smem] + [vmem] * (len(args) - 2),
        out_specs=(vmem, pl.BlockSpec(memory_space=pl.ANY)) if final else (vmem,),
        scratch_shapes=[pltpu.VMEM((K, 256), jnp.bfloat16)] * (2 * slots) + [pltpu.SemaphoreType.DMA((4,))] * final,
        input_output_aliases={} if acc is None else {4: 0},
        cost_estimate=pl.CostEstimate(flops=n * 450_000_000, bytes_accessed=n * 40_000, transcendentals=0),
        compiler_params=pltpu.CompilerParams(vmem_limit_bytes=16 << 20),
        name="finish" if final else "absorb",
    )(*args)
    return result[-1]


COORDS = ("x", "y", "zh", "zl", "core")


def permute(value, source):
    pairs = []
    for target in range(128):
        x, y, zh, zl, core = target // 32, target // 8 % 4, target // 4 % 2, target // 2 % 2, target % 2
        place = source(x, y, zh, zl, core)
        if place is not None:
            x, y, zh, zl, core = place
            pairs.append(((((x * 4 + y) * 2 + zh) * 2 + zl) * 2 + core, target))
    return lax.ppermute(value, COORDS, pairs)


def owner_at(steps):
    def source(x, y, zh, zl, core):
        owner = ((x * 4 + y) * 2 + zh + steps) % 32
        return owner // 8, owner // 2 % 4, owner % 2, zl, core

    return source


def after(value, *others):
    return lax.optimization_barrier((value, *others))


def local(walker_m, vertex_times, vertex_labels, freq_index, q_index):
    own, odd_freq = pack(freq_index, walker_m, vertex_times, vertex_labels)
    share = (2 * lax.axis_index("zl") + lax.axis_index("core")).astype(jnp.int32).reshape(1)

    def add(walkers, acc=None, final=False):
        return absorb(share, q_index, odd_freq, walkers, acc, final)

    def flip_zl(x, y, zh, zl, core):
        return x, y, zh, 1 - zl, core

    def flip_core(x, y, zh, zl, core):
        return x, y, zh, zl, 1 - core

    def flip_z(x, y, zh, zl, core):
        return x, y, 1 - zh, 1 - zl, core

    behind = permute(own, owner_at(-2))
    ahead = permute(own, owner_at(2))
    early = permute(own, flip_zl)
    own_far = permute(own, flip_core)
    acc = add(own)
    ahead, behind, early, own_far, acc = after(ahead, behind, early, own_far, acc)
    odd_owner = lax.axis_index("zh") == 1
    send = jnp.concatenate([own, jnp.where(odd_owner, behind, ahead)], axis=0)
    other = permute(send, flip_z)
    acc = add(jnp.concatenate([early, ahead, own_far], axis=0), acc)
    other, acc = after(other, acc)
    group = jnp.concatenate([ahead, other, early], axis=0)
    near = permute(group[0:3], flip_zl)
    group_far = permute(group, flip_core)
    acc = add(other, acc)
    group_far, acc = after(group_far, acc)
    acc = add(group_far, acc)
    near, acc = after(near, acc)
    near_far = permute(near, flip_core)
    acc = add(near, acc)
    near_far, acc = after(near_far, acc)
    return add(near_far, acc, True)[None]


def solution(mesh):
    fine = Mesh(mesh.devices.reshape(4, 4, 2, 2, 2), COORDS)
    walk, blk = ("zl", "core"), ("x", "y", "zh")
    return jax.shard_map(
        local,
        mesh=fine,
        in_specs=(P(walk, blk, None, None), P(walk, blk, None), P(walk, blk, None), P(), P(blk)),
        out_specs=P(blk, None, walk, None),
        check_vma=False,
    )
```
